256 devices in a mesh: comp: 8 (over x, core), tx: 8 (over z), ty: 4 (over y).
Axes of the slice: x: 4, y: 4, z: 8, core: 2. Of those that a mesh axis runs over, the one named last changes fastest.
Arguments:
- spectrum: float32 [1800, 64, 1024], P('comp', 'tx', 'ty'), may hold values from 0.05 to 2
- sea_mask: int32 [64, 1024], P('tx', 'ty'), may hold values from 0 to 1, as said below
- owner_list: int32 [8, 4, 64, 32], P('tx', 'ty'), may hold values from 0 to 2047, as said below
- owner_count: int32 [8, 4, 64], P('tx', 'ty'), may hold values from 0 to 32, as said below
- slopes: float32 [2, 64, 1024], P(None, 'tx', 'ty'), may hold values from -0.00015 to 0.00015
- friction: float32 [64, 1024], P('tx', 'ty'), may hold values from 0.15 to 0.6
- wind_angle: float32 [64, 1024], P('tx', 'ty'), may hold values from -3.140625 to 3.140625
Outputs:
- new_spectrum: float32 [1800, 64, 1024], P('comp', 'tx', 'ty')
The draws below stay inside these ranges and needn't reach their ends.
Inputs may be any that keep to these rules, and one draw needn't show every extreme that they name: `sea_mask`: 1 marks sea, 0 land. Each row of tiles along tx holds a tile without land, and each latitude row of a tile has a sea cell. `owner_list`: owner o is the device of index o along comp+tx (comp slowest) in the same row of tiles. For each tile, the first owner_count slots of each owner name cells of the tile as ix * 256 + iy; together they name every sea cell of the tile exactly once and no land cell. The other slots hold 0. `owner_count`: points of one tile given to one owner, at most 32; 32 is reached in every draw.
All inputs are finite; a program needn't handle non-finite values.
Results may differ from the reference program's by a relative error of at most 0.0003.
Values sent between devices are 32-bit elements; how exact they have to be, the bound alone decides.
A program may use at most 64 MiB of HBM per device.

```python
import math
import jax
import jax.numpy as jnp
from jax import lax

NDIR = 36
NFREQ = 50
CX = 8
CY = 256
KTOT = 1800
NX = 64
NY = 1024
CELLS = 2048
OWNERS = 64
CAP = 32
TX_TILES = 8
TY_TILES = 4


def coast_layout(key):
    base_key = jax.random.fold_in(key, 4177)
    key_list = jax.random.split(base_key, 5)
    widest = jax.random.randint(key_list[0], (TX_TILES, TY_TILES), 0, CX)
    open_tile = jax.random.randint(key_list[1], (TY_TILES,), 0, TX_TILES)
    widest = jnp.where(jnp.arange(TX_TILES, dtype=jnp.int32)[:, None] == open_tile[None, :], 0, widest)
    shore_width = jax.random.randint(key_list[2], (TX_TILES, TY_TILES, CY), 0, widest[:, :, None] + 1)
    column_ids = jnp.arange(CX, dtype=jnp.int32)[None, None, :, None]
    sea_tile = (column_ids >= shore_width[:, :, None, :]).astype(jnp.int32)
    sea_flat = sea_tile.reshape(TX_TILES * TY_TILES, CELLS)
    tile_keys = jax.random.split(key_list[3], TX_TILES * TY_TILES)

    def tile_ranks(tile_key):
        return jax.random.permutation(tile_key, CELLS).astype(jnp.int32)
    shuffled = jax.vmap(tile_ranks)(tile_keys)
    offsets = jax.random.randint(key_list[4], (TX_TILES * TY_TILES,), 0, OWNERS)
    positions = jnp.arange(CELLS, dtype=jnp.int32)
    owner_ids = jnp.arange(OWNERS, dtype=jnp.int32)

    def one_tile(sea_row, ranks, shift_by):
        order_key = (1 - sea_row) * CELLS + ranks
        ordering = jnp.argsort(order_key, stable=True).astype(jnp.int32)
        sea_total = jnp.sum(sea_row)
        owner_of = (positions + shift_by) % OWNERS
        slot_index = owner_of * CAP + positions // OWNERS
        target = jnp.where(positions < sea_total, slot_index, OWNERS * CAP)
        cell_names = jnp.zeros((OWNERS * CAP,), jnp.int32).at[target].set(ordering, mode='drop')
        taken = ((positions < sea_total)[:, None] & (owner_of[:, None] == owner_ids[None, :])).astype(jnp.int32)
        return (cell_names.reshape(OWNERS, CAP), jnp.sum(taken, axis=0))
    name_lists, count_lists = jax.vmap(one_tile)(sea_flat, shuffled, offsets)
    sea_grid = sea_tile.transpose(0, 2, 1, 3).reshape(TX_TILES * CX, TY_TILES * CY)
    return (sea_grid, name_lists.reshape(TX_TILES, TY_TILES, OWNERS, CAP), count_lists.reshape(TX_TILES, TY_TILES, OWNERS))


def draw_sea_mask(key, part):
    return coast_layout(key)[0]


def draw_owner_list(key, part):
    return coast_layout(key)[1]


def draw_owner_count(key, part):
    return coast_layout(key)[2]


def level_of(own_key, extent, pieces, smallest, top_value):
    level = 1.0
    for position, shards_of in pieces:
        steps = jax.random.uniform(jax.random.fold_in(jax.random.fold_in(own_key, 6), position), (shards_of,), jnp.float32, smallest / len(pieces), top_value / len(pieces))
        level = level * jnp.repeat(jnp.exp(steps), extent[position] // shards_of).reshape((-1,) + (1,) * (len(extent) - 1 - position))
    return level


def setup_inputs(seed: int = 0) -> dict:
    key_of = jax.random.split(jax.random.key(seed), 8)
    spectrum = jnp.clip(jnp.exp(math.log(2.0) - 3.6888794 * jax.random.uniform(key_of[0], (KTOT, NX, NY), jnp.float32) ** level_of(key_of[0], (KTOT, NX, NY), ((0, 8), (1, 8), (2, 4)), -0.2, 0.2)), 0.05, 2.0)
    sea_mask = draw_sea_mask(jax.random.fold_in(key_of[7], 71), 0)
    owner_list = draw_owner_list(jax.random.fold_in(key_of[7], 71), 0)
    owner_count = draw_owner_count(jax.random.fold_in(key_of[7], 71), 0)
    slopes = jnp.clip(jax.random.uniform(key_of[4], (2, NX, NY), jnp.float32, -0.00015, 0.00015) * level_of(key_of[4], (2, NX, NY), ((1, 8), (2, 4)), -0.4, 0.0), -0.00015, 0.00015)
    friction = jnp.clip(0.15 + 0.45000002 * jax.random.uniform(key_of[5], (NX, NY), jnp.float32) ** level_of(key_of[5], (NX, NY), ((0, 8), (1, 4)), -0.2, 0.2), 0.15, 0.6)
    wind_angle = jnp.clip(jax.random.uniform(key_of[6], (NX, NY), jnp.float32, -3.140625, 3.140625), -3.140625, 3.140625)
    return {"spectrum": spectrum, "sea_mask": sea_mask, "owner_list": owner_list, "owner_count": owner_count, "slopes": slopes, "friction": friction, "wind_angle": wind_angle}


TIME_STEP = 240.0
CELL_SIZE = 11100.0
GRAVITY = 9.81
LOW_FREQ = 0.0373
HIGH_FREQ = 1.0
WIND_GROWTH = 1e-4
WIND_FACTOR = 28.0
SATURATION_LOSS = 5e-4
CUMULATIVE_LOSS = 1e-3
STEEPNESS_LOSS = 5e-3
SATURATION_LEVEL = 0.6


def freq_values(freq_ids):
    return (2.0 * math.pi * LOW_FREQ) * jnp.exp(freq_ids.astype(jnp.float32) * (math.log(HIGH_FREQ / LOW_FREQ) / (NFREQ - 1)))


def wave_tables(first_comp, comp_count):
    comp_ids = first_comp + jnp.arange(comp_count, dtype=jnp.int32)
    headings = (comp_ids // NFREQ).astype(jnp.float32) * (2.0 * math.pi / NDIR)
    return headings, freq_values(comp_ids % NFREQ)


def advect(energy, west_side, east_side, south_side, north_side, prev_dir, next_dir, headings, ang_freq, slopes):
    group_speed = GRAVITY / (2.0 * ang_freq)
    along_x = ((TIME_STEP / CELL_SIZE) * group_speed * jnp.cos(headings))[:, None, None]
    along_y = ((TIME_STEP / CELL_SIZE) * group_speed * jnp.sin(headings))[:, None, None]
    bending = (TIME_STEP * NDIR / (2.0 * math.pi)) * (2.0 * math.pi * LOW_FREQ) / ang_freq
    turning = bending[:, None, None] * (jnp.sin(headings)[:, None, None] * slopes[0][None] - jnp.cos(headings)[:, None, None] * slopes[1][None])
    change = jnp.maximum(along_x, 0.0) * (energy - west_side) + jnp.minimum(along_x, 0.0) * (east_side - energy)
    change = change + jnp.maximum(along_y, 0.0) * (energy - south_side) + jnp.minimum(along_y, 0.0) * (north_side - energy)
    change = change + jnp.maximum(turning, 0.0) * (energy - prev_dir) + jnp.minimum(turning, 0.0) * (next_dir - energy)
    return energy - change


def source_terms(spectra, friction, wind_angle):
    dir_ids = jnp.arange(NDIR, dtype=jnp.int32)
    offset = (dir_ids[:, None] - dir_ids[None, :]) % NDIR
    nearest = jnp.minimum(offset, NDIR - offset)
    spread = jnp.where(4 * nearest < NDIR, jnp.cos(offset.astype(jnp.float32) * (2.0 * math.pi / NDIR)) ** 2, 0.0)
    spread = spread / jnp.sum(spread, axis=1, keepdims=True)
    sat_level = jnp.einsum("de,efp->dfp", spread, spectra, precision=lax.Precision.HIGHEST)
    excess = jnp.maximum(sat_level / SATURATION_LEVEL - 1.0, 0.0)
    excess_sq = excess * excess
    freq_ids = jnp.arange(NFREQ, dtype=jnp.int32)
    below_mask = (freq_ids[None, :] < freq_ids[:, None]).astype(jnp.float32)
    running = jnp.einsum("fg,dgp->dfp", below_mask, excess_sq, precision=lax.Precision.HIGHEST) / NFREQ
    ang_freq = freq_values(freq_ids)
    weights = (ang_freq / ang_freq[NFREQ - 1]) ** 2
    steepness = jnp.einsum("dfp,f->p", spectra, weights, precision=lax.Precision.HIGHEST) / (NDIR * NFREQ)
    headings = dir_ids.astype(jnp.float32) * (2.0 * math.pi / NDIR)
    alignment = jnp.cos(headings)[:, None, None] * jnp.cos(wind_angle)[None, None, :] + jnp.sin(headings)[:, None, None] * jnp.sin(wind_angle)[None, None, :]
    forcing = (WIND_FACTOR / GRAVITY) * friction[None, None, :] * ang_freq[None, :, None] * alignment
    growth = WIND_GROWTH * ang_freq[None, :, None] * jnp.maximum(forcing - 1.0, 0.0)
    losses = ang_freq[None, :, None] * (SATURATION_LOSS * excess_sq + CUMULATIVE_LOSS * running + STEEPNESS_LOSS * (steepness * steepness)[None, None, :])
    return spectra * (1.0 + TIME_STEP * growth) / (1.0 + TIME_STEP * losses)


def listed_cells(owner_list, owner_count):
    slot_ids = jnp.arange(CAP, dtype=jnp.int32)

    def one_tile(cell_names, counts_here):
        in_use = slot_ids[None, :] < counts_here[:, None]
        target = jnp.where(in_use, cell_names, CELLS).reshape(-1)
        listed = jnp.zeros((CELLS,), jnp.int32).at[target].set(1, mode="drop")
        return listed.reshape(CX, CY)

    per_tile = jax.vmap(jax.vmap(one_tile))(owner_list, owner_count)
    return per_tile.transpose(0, 2, 1, 3).reshape(NX, NY)


def reference(spectrum, sea_mask, owner_list, owner_count, slopes, friction, wind_angle):
    sea_cells = sea_mask.astype(jnp.float32)
    masked = spectrum * sea_cells[None]

    def one_heading(heading):
        first_comp = heading * NFREQ
        centre = lax.dynamic_slice_in_dim(masked, first_comp, NFREQ, 0)
        prev_dir = lax.dynamic_slice_in_dim(masked, ((heading + NDIR - 1) % NDIR) * NFREQ, NFREQ, 0)
        next_dir = lax.dynamic_slice_in_dim(masked, ((heading + 1) % NDIR) * NFREQ, NFREQ, 0)
        west_side = jnp.roll(centre, 1, axis=1)
        east_side = jnp.roll(centre, -1, axis=1)
        south_side = jnp.pad(centre, ((0, 0), (0, 0), (1, 0)))[:, :, :-1]
        north_side = jnp.pad(centre, ((0, 0), (0, 0), (0, 1)))[:, :, 1:]
        headings, ang_freq = wave_tables(first_comp, NFREQ)
        advected = advect(centre, west_side, east_side, south_side, north_side, prev_dir, next_dir, headings, ang_freq, slopes)
        return advected * sea_cells[None]

    advected = lax.map(one_heading, jnp.arange(NDIR, dtype=jnp.int32)).reshape(NDIR * NFREQ, NX, NY)

    def one_row(row_index):
        column = lax.dynamic_index_in_dim(advected, row_index, 1, keepdims=False)
        result = source_terms(column.reshape(NDIR, NFREQ, NY), friction[row_index], wind_angle[row_index])
        return result.reshape(NDIR * NFREQ, NY)

    updated = jnp.moveaxis(lax.map(one_row, jnp.arange(NX, dtype=jnp.int32)), 0, 1)
    listed = listed_cells(owner_list, owner_count)
    return jnp.where(listed[None] > 0, updated, advected)
```

```python
import math

import jax
import jax.numpy as jnp
import numpy as np
from jax import lax
from jax.experimental import pallas as pl
from jax.experimental.pallas import tpu as pltpu
from jax.sharding import PartitionSpec as P

NDIR = 36
NFREQ = 50
HALF = 25
OWN = 9
REACH = 16
ROWS = 8
COLS = 256
TALL = HALF * ROWS
PACK = 32

TIME_STEP = 240.0
CELL_SIZE = 11100.0
GRAVITY = 9.81
LOW_FREQ = 0.0373
HIGH_FREQ = 1.0
WIND_GROWTH = 0.0001
WIND_FACTOR = 28.0
SATURATION_LOSS = 0.0005
CUMULATIVE_LOSS = 0.001
STEEPNESS_LOSS = 0.005
SATURATION_LEVEL = 0.6

T_COS, T_SIN, T_SPEED, T_BEND, T_OMEGA, T_STEEP = 0, 36, 72, 122, 172, 222


def tables():
    heading = 2.0 * math.pi / NDIR * np.arange(NDIR)
    omega = 2.0 * math.pi * LOW_FREQ * (HIGH_FREQ / LOW_FREQ) ** (np.arange(NFREQ) / (NFREQ - 1))
    speed = TIME_STEP / CELL_SIZE * GRAVITY / (2.0 * omega)
    bend = TIME_STEP * NDIR / (2.0 * math.pi) * (2.0 * math.pi * LOW_FREQ) / omega
    steep = (omega / omega[-1]) ** 2 / (NDIR * NFREQ)
    return np.concatenate([np.cos(heading), np.sin(heading), speed, bend, omega, steep]).astype(
        np.float32
    )


def spread_weights():
    weights = np.cos(2.0 * math.pi / NDIR * np.arange(REACH // 2 + 1)) ** 2
    total = weights[0] + 2.0 * np.sum(weights[1:])
    return [float(w) for w in weights / total / SATURATION_LEVEL]


def kernel(
    spec,
    table,
    sea_mask,
    slopes,
    friction,
    wind,
    out,
    raw,
    moved,
    lon_out,
    lon_in,
    lat_out,
    lat_in,
    steep,
    offset,
    own_sem,
    raw_send,
    raw_recv,
    lon_send,
    lon_recv,
    lat_send,
    lat_recv,
    near_send,
    link_send,
    far_send,
    relay_send,
    block_recv,
    steep_send,
    steep_recv,
    offset_send,
    offset_recv,
):
    comp = lax.axis_index("comp")
    tx = lax.axis_index("tx")
    ty = lax.axis_index("ty")
    parity = comp % 2
    quadrant = comp // 2
    pos_x = 1 - ((quadrant + 1) // 2) % 2
    pos_y = 1 - quadrant // 2

    def at_comp(step):
        return {"comp": (comp + step + 8) % 8}

    def remote(src, dst, send, recv, device):
        return pltpu.make_async_remote_copy(
            src_ref=src,
            dst_ref=dst,
            send_sem=send,
            recv_sem=recv,
            device_id=device,
            device_id_type=pl.DeviceIdType.MESH,
        )

    load_own = pltpu.make_async_copy(spec, raw.at[2 : 2 + OWN], own_sem)
    load_own.start()
    barrier = pltpu.get_barrier_semaphore()
    for step in range(1, 8):
        pl.semaphore_signal(
            barrier, inc=1, device_id=at_comp(step), device_id_type=pl.DeviceIdType.MESH
        )
    for step in (1, -1):
        pl.semaphore_signal(
            barrier,
            inc=1,
            device_id={"tx": (tx + step + 8) % 8},
            device_id_type=pl.DeviceIdType.MESH,
        )
        pl.semaphore_signal(
            barrier,
            inc=1,
            device_id={"ty": (ty + step + 4) % 4},
            device_id_type=pl.DeviceIdType.MESH,
        )

    sea = sea_mask[...].astype(jnp.float32)
    row_ids = lax.broadcasted_iota(jnp.int32, (ROWS, COLS), 0)
    lane_ids = lax.broadcasted_iota(jnp.int32, (ROWS, 128), 1)
    inflow_row = jnp.where(row_ids == (1 - pos_x) * (ROWS - 1), 1.0, 0.0) > 0.5
    inflow_lane = jnp.where(lane_ids == (1 - pos_y) * 127, 1.0, 0.0) > 0.5
    up_y = jnp.zeros((ROWS, 128), jnp.int32) + pos_y > 0
    row_shift = jnp.where(pos_x > 0, 1, ROWS - 1)
    lane_shift = jnp.where(pos_y > 0, 1, 127)

    last_row = pos_x * (ROWS - 1)
    last_lane = pos_y * 127
    last_half = pl.multiple_of(pos_y * 128, 128)
    sea_row = jnp.sum(jnp.where(row_ids == last_row, sea, 0.0), axis=0, keepdims=True)
    sea_half = jnp.where(up_y, sea[:, 128:], sea[:, :128])

    load_own.wait()

    def first_block(phase):
        return (phase + parity) % 2

    def pack(phase):
        first = first_block(phase)

        def pack_block(t, carry):
            block = first + 2 * t
            lon_out[phase, t, pl.ds(PACK - ROWS, ROWS), :] = jnp.zeros((ROWS, COLS), jnp.float32)

            def pack_one(j, lat):
                lon_out[phase, t, pl.ds(j, 1), :] = (
                    raw[2 + block, pl.ds(ROWS * j + last_row, 1), :] * sea_row
                )
                side = raw[2 + block, pl.ds(pl.multiple_of(ROWS * j, ROWS), ROWS), pl.ds(last_half, 128)]
                turned = pltpu.roll(side * sea_half, (j - last_lane + 128) % 128, 1)
                return jnp.where(lane_ids == j, turned, lat)

            lat_out[phase, t] = lax.fori_loop(
                0, HALF, pack_one, jnp.zeros((ROWS, 128), jnp.float32), unroll=5
            )
            return carry

        lax.fori_loop(0, 5 - first, pack_block, 0)

    lat_out[...] = jnp.zeros(lat_out.shape, jnp.float32)
    pack(0)
    pl.semaphore_wait(barrier, 11)

    def raw_copies(phase):
        first = first_block(phase)
        return [
            remote(
                raw.at[2 + first],
                raw.at[11 + first],
                raw_send.at[phase, 0],
                raw_recv.at[phase, 0],
                at_comp(-1),
            ),
            remote(
                raw.at[10 - first],
                raw.at[1 - first],
                raw_send.at[phase, 1],
                raw_recv.at[phase, 1],
                at_comp(1),
            ),
        ]

    lon_to = {"tx": (tx + 2 * pos_x - 1 + 8) % 8}
    lat_to = {"ty": (ty + 2 * pos_y - 1 + 4) % 4}

    def lon_copy(phase, start, count, which):
        return remote(
            lon_out.at[phase, start : start + count],
            lon_in.at[phase, start : start + count],
            lon_send.at[phase, which],
            lon_recv.at[phase, which],
            lon_to,
        )

    def lat_copy(phase):
        return remote(
            lat_out.at[phase], lat_in.at[phase], lat_send.at[phase], lat_recv.at[phase], lat_to
        )

    def send_halos(phase):
        for copy in raw_copies(phase):
            copy.start()
        lon_copy(phase, 0, 4, 0).start()

        @pl.when(first_block(phase) == 0)
        def _():
            lon_copy(phase, 4, 1, 1).start()

        lat_copy(phase).start()

    def wait_halos(phase):
        for copy in raw_copies(phase):
            copy.wait_send()
        first = first_block(phase)
        remote(raw.at[2], raw.at[12 - first], raw_send.at[phase, 0], raw_recv.at[phase, 0], at_comp(1)).wait_recv()
        remote(raw.at[2], raw.at[first], raw_send.at[phase, 1], raw_recv.at[phase, 1], at_comp(1)).wait_recv()
        lon_copy(phase, 0, 4, 0).wait()

        @pl.when(first_block(phase) == 0)
        def _():
            lon_copy(phase, 4, 1, 1).wait()

        lat_copy(phase).wait()

    lat_open = jnp.where(pos_y > 0, ty, 3 - ty) > 0
    lat_gate = jnp.where(lat_open, 1.0, 0.0)
    slope_x = slopes[0]
    slope_y = slopes[1]

    def advect(phase, steepness):
        first = first_block(phase)

        def one_block(t, steepness):
            block = first + 2 * t
            place = OWN * comp + block
            heading = place // 2
            freq = HALF * (place % 2)
            cos = table[T_COS + heading]
            sin = table[T_SIN + heading]
            abs_cos = jnp.abs(cos)
            abs_sin = jnp.abs(sin)
            bend_x = sin * slope_x - cos * slope_y
            lat = lat_in[phase, t] * lat_gate

            def one(j, steepness):
                rows = pl.ds(pl.multiple_of(ROWS * j, ROWS), ROWS)
                centre = raw[2 + block, rows, :]
                prev_dir = raw[block, rows, :]
                next_dir = raw[4 + block, rows, :]
                masked = centre * sea
                up_lon = jnp.where(
                    inflow_row,
                    jnp.broadcast_to(lon_in[phase, t, pl.ds(j, 1), :], (ROWS, COLS)),
                    pltpu.roll(masked, row_shift, 0),
                )
                side = pltpu.roll(lat, (last_lane_in - j + 128) % 128, 1)
                low = pltpu.roll(masked[:, :128], lane_shift, 1)
                high = pltpu.roll(masked[:, 128:], lane_shift, 1)
                low_up = jnp.where(inflow_lane, jnp.where(up_y, side, high), low)
                high_up = jnp.where(inflow_lane, jnp.where(up_y, low, side), high)
                up_lat = jnp.concatenate([low_up, high_up], axis=1)
                speed = table[T_SPEED + freq + j]
                turning = table[T_BEND + freq + j] * bend_x
                value = sea * (
                    centre
                    - (speed * abs_cos) * (centre - up_lon)
                    - (speed * abs_sin) * (centre - up_lat)
                    - (
                        jnp.maximum(turning, 0.0) * (centre - prev_dir)
                        + jnp.minimum(turning, 0.0) * (next_dir - centre)
                    )
                )
                moved[REACH + block, rows, :] = value
                return steepness + table[T_STEEP + freq + j] * value

            return lax.fori_loop(0, HALF, one, steepness, unroll=5)

        return lax.fori_loop(0, 5 - first, one_block, steepness)

    last_lane_in = (1 - pos_y) * 127

    def shifted(side, phase, action):
        first = (phase + side) % 2
        mine = list(range(first, OWN, 2))
        far = [b for b in mine if (b >= 2 if side == 0 else b <= 6)]
        theirs = list(range(1 - first, OWN, 2))
        relay = [b for b in theirs if (b >= 2 if side == 0 else b <= 6)]
        link = [b for b in mine if (b <= 6 if side == 0 else b >= 2)]
        link += [b for b in mine if b not in link]
        partner, other = (1, -1) if side == 0 else (-1, 1)

        def block_copy(src, dst, sems, device):
            return remote(moved.at[src], moved.at[dst], sems.at[src], block_recv.at[dst], device)

        def arrived(dst):
            block_copy(REACH, dst, near_send, at_comp(1)).wait_recv()

        links = [
            block_copy(REACH + b, REACH + b - OWN * other, link_send, at_comp(other)) for b in link
        ]
        fars = [
            block_copy(REACH + b, REACH + b - 2 * OWN * partner, far_send, at_comp(2 * partner))
            for b in far
        ]
        nears = [
            block_copy(REACH + b, REACH + b - OWN * partner, near_send, at_comp(partner))
            for b in mine
        ]
        relay_from = [REACH + b + OWN * other for b in relay]
        relays = [
            block_copy(src, src - OWN * partner, relay_send, at_comp(partner)) for src in relay_from
        ]
        if action == "send":
            for copy in links + fars + nears:
                copy.start()
        elif action == "relay":
            for src, copy in zip(relay_from, relays):
                arrived(src)
                copy.start()
        elif action == "receive":
            for b in theirs:
                arrived(REACH + b + OWN * partner)
                if b not in relay:
                    arrived(REACH + b + OWN * other)
            for b in mine:
                if b in far:
                    pass
            far_in = [b for b in mine if (b >= 2 if side == 0 else b <= 6)]
            for b in far_in:
                arrived(REACH + b - 2 * OWN * partner)
            for b in mine:
                if b <= 6 if side == 0 else b >= 2:
                    arrived(REACH + b + 2 * OWN * partner)
        else:
            for copy in links + fars + nears + relays:
                copy.wait_send()

    def exchange(phase, action):
        for side in (0, 1):

            @pl.when(parity == side)
            def _():
                shifted(side, phase, action)

    def steep_copy(step):
        return remote(
            steep.at[comp], steep.at[comp], steep_send.at[step], steep_recv.at[comp], at_comp(step)
        )

    send_halos(0)
    pack(1)
    send_halos(1)
    wait_halos(0)
    partial = advect(0, jnp.zeros((ROWS, COLS), jnp.float32))
    exchange(0, "send")
    wait_halos(1)
    partial = advect(1, partial)
    exchange(1, "send")
    steep[comp] = partial
    for step in range(1, 8):
        steep_copy(step).start()

    weights = spread_weights()
    wind_x = (WIND_FACTOR / GRAVITY) * friction[...] * jnp.cos(wind[...])
    wind_y = (WIND_FACTOR / GRAVITY) * friction[...] * jnp.sin(wind[...])

    for step in range(1, 8):
        slot = (comp + step) % 8
        remote(
            steep.at[slot], steep.at[slot], steep_send.at[step], steep_recv.at[slot], at_comp(step)
        ).wait_recv()
    total = steep[0]
    for slot in range(1, 8):
        total = total + steep[slot]
    steep_loss = (TIME_STEP * STEEPNESS_LOSS) * total * total
    at_sea = sea > 0.5

    def sources(phase):
        first = first_block(phase)

        def one_block(t, carry):
            block = first + 2 * t
            place = OWN * comp + block
            heading = place // 2
            freq = HALF * (place % 2)
            cos = table[T_COS + heading]
            sin = table[T_SIN + heading]
            along = cos * wind_x + sin * wind_y

            def one(j, running):
                rows = pl.ds(pl.multiple_of(ROWS * j, ROWS), ROWS)
                centre = moved[REACH + block, rows, :]
                level = weights[0] * centre
                for m in range(1, REACH // 2 + 1):
                    level = level + weights[m] * (
                        moved[REACH + block - 2 * m, rows, :] + moved[REACH + block + 2 * m, rows, :]
                    )
                excess = jnp.maximum(level - 1.0, 0.0)
                excess_sq = excess * excess
                omega = table[T_OMEGA + freq + j]
                growth = (TIME_STEP * WIND_GROWTH * omega) * jnp.maximum(omega * along - 1.0, 0.0)
                losses = omega * (
                    (TIME_STEP * SATURATION_LOSS) * excess_sq
                    + (TIME_STEP * CUMULATIVE_LOSS / NFREQ) * running
                    + steep_loss
                )
                updated = centre * (1.0 + growth) / (1.0 + losses)
                out[block, rows, :] = jnp.where(at_sea, updated, centre)
                return running + excess_sq

            if phase == 0:
                start = jnp.zeros((ROWS, COLS), jnp.float32)
            else:
                start = offset[block]
            offset[block + 1] = lax.fori_loop(0, HALF, one, start, unroll=5)
            return carry

        lax.fori_loop(0, 5 - first, one_block, 0)

    offset_copy = remote(
        offset.at[OWN], offset.at[0], offset_send, offset_recv, {"comp": comp + 1 - 2 * parity}
    )
    exchange(0, "relay")
    exchange(0, "receive")
    sources(0)

    @pl.when(parity == 0)
    def _():
        offset_copy.start()

    exchange(1, "relay")
    exchange(1, "receive")

    @pl.when(parity == 1)
    def _():
        offset_copy.wait_recv()

    sources(1)

    @pl.when(parity == 0)
    def _():
        offset_copy.wait_send()

    exchange(0, "drain")
    exchange(1, "drain")
    for step in range(1, 8):
        steep_copy(step).wait_send()


def shards(spectrum, sea_mask, owner_list, owner_count, slopes, friction, wind_angle):
    blocks = spectrum.reshape(OWN, TALL, COLS)
    vmem = pl.BlockSpec(memory_space=pltpu.VMEM)
    dma = pltpu.SemaphoreType.DMA
    result = pl.pallas_call(
        kernel,
        out_shape=jax.ShapeDtypeStruct((OWN, TALL, COLS), jnp.float32),
        in_specs=[
            pl.BlockSpec(memory_space=pl.ANY),
            pl.BlockSpec(memory_space=pltpu.SMEM),
            vmem,
            vmem,
            vmem,
            vmem,
        ],
        out_specs=vmem,
        scratch_shapes=[
            pltpu.VMEM((OWN + 4, TALL, COLS), jnp.float32),
            pltpu.VMEM((OWN + 2 * REACH, TALL, COLS), jnp.float32),
            pltpu.VMEM((2, 5, PACK, COLS), jnp.float32),
            pltpu.VMEM((2, 5, PACK, COLS), jnp.float32),
            pltpu.VMEM((2, 5, ROWS, 128), jnp.float32),
            pltpu.VMEM((2, 5, ROWS, 128), jnp.float32),
            pltpu.VMEM((8, ROWS, COLS), jnp.float32),
            pltpu.VMEM((OWN + 1, ROWS, COLS), jnp.float32),
            dma,
            dma((2, 2)),
            dma((2, 2)),
            dma((2, 2)),
            dma((2, 2)),
            dma((2,)),
            dma((2,)),
            dma((OWN + 2 * REACH,)),
            dma((OWN + 2 * REACH,)),
            dma((OWN + 2 * REACH,)),
            dma((OWN + 2 * REACH,)),
            dma((OWN + 2 * REACH,)),
            dma((8,)),
            dma((8,)),
            dma,
            dma,
        ],
        compiler_params=pltpu.CompilerParams(
            collective_id=0, has_side_effects=True, vmem_limit_bytes=40 << 20
        ),
        name="wave_step",
    )(blocks, jnp.asarray(tables()), sea_mask, slopes, friction, wind_angle)
    return result.reshape(spectrum.shape)


def solution(mesh):
    in_specs = (
        P("comp", "tx", "ty"),
        P("tx", "ty"),
        P("tx", "ty", None, None),
        P("tx", "ty", None),
        P(None, "tx", "ty"),
        P("tx", "ty"),
        P("tx", "ty"),
    )
    out_specs = P("comp", "tx", "ty")
    return jax.shard_map(shards, mesh=mesh, in_specs=in_specs, out_specs=out_specs, check_vma=False)
```

```python
import math

import jax
import jax.numpy as jnp
import numpy as np
from jax import lax
from jax.experimental import pallas as pl
from jax.experimental.pallas import tpu as pltpu
from jax.sharding import PartitionSpec as P

NDIR = 36
NFREQ = 50
HALF = 25
OWN = 9
REACH = 16
ROWS = 8
COLS = 256
TALL = HALF * ROWS
PHASES = ((0, 0, 5), (0, 5, 10), (0, 15, 10), (1, 0, 10), (1, 10, 10), (1, 20, 5))
EARLY = 3

TIME_STEP = 240.0
CELL_SIZE = 11100.0
GRAVITY = 9.81
LOW_FREQ = 0.0373
HIGH_FREQ = 1.0
WIND_GROWTH = 0.0001
WIND_FACTOR = 28.0
SATURATION_LOSS = 0.0005
CUMULATIVE_LOSS = 0.001
STEEPNESS_LOSS = 0.005
SATURATION_LEVEL = 0.6

T_COS, T_SIN, T_SPEED, T_BEND, T_OMEGA, T_STEEP, T_END = 0, 36, 72, 122, 172, 222, 272


def tables():
    heading = 2.0 * math.pi / NDIR * np.arange(NDIR)
    omega = 2.0 * math.pi * LOW_FREQ * (HIGH_FREQ / LOW_FREQ) ** (np.arange(NFREQ) / (NFREQ - 1))
    speed = TIME_STEP / CELL_SIZE * GRAVITY / (2.0 * omega)
    bend = TIME_STEP * NDIR / (2.0 * math.pi) * (2.0 * math.pi * LOW_FREQ) / omega
    steep = (omega / omega[-1]) ** 2 / (NDIR * NFREQ)
    return np.concatenate([np.cos(heading), np.sin(heading), speed, bend, omega, steep]).astype(
        np.float32
    )


def spread_weights():
    weights = np.cos(2.0 * math.pi / NDIR * np.arange(REACH // 2 + 1)) ** 2
    total = weights[0] + 2.0 * np.sum(weights[1:])
    return [float(w) for w in weights / total / SATURATION_LEVEL]


def lon_rows(phase):
    return (5 * PHASES[phase][2] + ROWS - 1) // ROWS * ROWS


def lon_base(phase):
    return sum(lon_rows(p) for p in range(phase))


def kernel(
    spec,
    table_in,
    sea_in,
    slopes_in,
    friction_in,
    wind_in,
    out,
    raw,
    moved,
    lon_out,
    lon_in,
    lat_out,
    lat_in,
    steep,
    offset,
    table,
    sea_mask,
    slopes,
    friction,
    wind,
    load_sem,
    raw_send,
    raw_recv,
    lon_send,
    lon_recv,
    lat_send,
    lat_recv,
    block_send,
    block_recv,
    steep_send,
    steep_recv,
    offset_send,
    offset_recv,
):
    comp = lax.axis_index("comp")
    tx = lax.axis_index("tx")
    ty = lax.axis_index("ty")
    parity = comp % 2
    quadrant = comp // 2
    pos_x = 1 - ((quadrant + 1) // 2) % 2
    pos_y = 1 - quadrant // 2

    def at_comp(step):
        return {"comp": (comp + step + 8) % 8}

    def remote(src, dst, send, recv, device):
        return pltpu.make_async_remote_copy(
            src_ref=src,
            dst_ref=dst,
            send_sem=send,
            recv_sem=recv,
            device_id=device,
            device_id_type=pl.DeviceIdType.MESH,
        )

    barrier = pltpu.get_barrier_semaphore()

    def greet(device):
        pl.semaphore_signal(barrier, inc=1, device_id=device, device_id_type=pl.DeviceIdType.MESH)

    for step in (4, 3, 5, 2, 6, 1, 7):
        greet(at_comp(step))
    for step in (1, -1):
        greet({"tx": (tx + step + 8) % 8})
        greet({"ty": (ty + step + 4) % 4})

    pairs = [
        (sea_in, sea_mask),
        (spec, raw.at[2 : 2 + OWN]),
        (table_in, table),
        (slopes_in, slopes),
        (friction_in, friction),
        (wind_in, wind),
    ]
    loads = [pltpu.make_async_copy(src, dst, load_sem.at[i]) for i, (src, dst) in enumerate(pairs)]
    for load in loads:
        load.start()

    row_ids = lax.broadcasted_iota(jnp.int32, (ROWS, COLS), 0)
    lane_ids = lax.broadcasted_iota(jnp.int32, (ROWS, 128), 1)
    inflow_row = row_ids == (1 - pos_x) * (ROWS - 1)
    last_lane_in = (1 - pos_y) * 127
    inflow_lane = lane_ids == last_lane_in
    up_y = jnp.zeros((ROWS, 128), jnp.int32) + pos_y > 0
    row_shift = jnp.where(pos_x > 0, 1, ROWS - 1)
    lane_shift = jnp.where(pos_y > 0, 1, 127)
    last_row = pos_x * (ROWS - 1)
    last_lane = pos_y * 127
    last_half = pl.multiple_of(pos_y * 128, 128)

    for load in loads:
        load.wait()
    sea = sea_mask[...].astype(jnp.float32)
    sea_row = jnp.sum(jnp.where(row_ids == last_row, sea, 0.0), axis=0, keepdims=True)
    sea_half = jnp.where(up_y, sea[:, 128:], sea[:, :128])

    def first_block(phase):
        return (PHASES[phase][0] + parity) % 2

    def span(phase):
        _, start, count = PHASES[phase]
        return pl.ds(ROWS * start, ROWS * count)

    def pack(phase):
        _, start, count = PHASES[phase]
        first = first_block(phase)

        def pack_block(t, carry):
            block = first + 2 * t

            def pack_one(i, lat):
                j = start + i
                lon_out[pl.ds(lon_base(phase) + count * t + i, 1), :] = (
                    raw[2 + block, pl.ds(ROWS * j + last_row, 1), :] * sea_row
                )
                rows = pl.ds(pl.multiple_of(ROWS * j, ROWS), ROWS)
                side = raw[2 + block, rows, pl.ds(last_half, 128)]
                turned = pltpu.roll(side * sea_half, (j - last_lane + 128) % 128, 1)
                return jnp.where(lane_ids == j, turned, lat)

            lat_out[phase, t] = lax.fori_loop(
                0, count, pack_one, jnp.zeros((ROWS, 128), jnp.float32), unroll=5
            )
            return carry

        lax.fori_loop(0, 5 - first, pack_block, 0)

    def raw_copies(phase):
        first = first_block(phase)
        rows = span(phase)
        return [
            remote(
                spec.at[first, rows],
                raw.at[11 + first, rows],
                raw_send,
                raw_recv.at[phase],
                at_comp(-1),
            ),
            remote(
                spec.at[8 - first, rows],
                raw.at[1 - first, rows],
                raw_send,
                raw_recv.at[phase],
                at_comp(1),
            ),
        ]

    lon_to = {"tx": (tx + 2 * pos_x - 1 + 8) % 8}
    lat_to = {"ty": (ty + 2 * pos_y - 1 + 4) % 4}

    def lon_copy(phase):
        rows = pl.ds(lon_base(phase), lon_rows(phase))
        return remote(lon_out.at[rows], lon_in.at[rows], lon_send, lon_recv.at[phase], lon_to)

    def lat_copy(phase):
        return remote(lat_out.at[phase], lat_in.at[phase], lat_send, lat_recv.at[phase], lat_to)

    def wait_halos(phase):
        both = raw.at[0:2, span(phase)]
        remote(both, both, raw_send, raw_recv.at[phase], at_comp(1)).wait_recv()
        lon_copy(phase).wait_recv()
        lat_copy(phase).wait_recv()

    lat_open = jnp.where(pos_y > 0, ty, 3 - ty) > 0
    lat_gate = jnp.where(lat_open, 1.0, 0.0)
    slope_x = slopes[0]
    slope_y = slopes[1]

    def advect(phase, steepness):
        _, start, count = PHASES[phase]
        first = first_block(phase)

        def one_block(t, steepness):
            block = first + 2 * t
            place = OWN * comp + block
            heading = place // 2
            freq = HALF * (place % 2)
            cos = table[T_COS + heading]
            sin = table[T_SIN + heading]
            abs_cos = jnp.abs(cos)
            abs_sin = jnp.abs(sin)
            bend_x = sin * slope_x - cos * slope_y
            lat = lat_in[phase, t] * lat_gate

            def one(i, steepness):
                j = start + i
                rows = pl.ds(pl.multiple_of(ROWS * j, ROWS), ROWS)
                centre = raw[2 + block, rows, :]
                prev_dir = raw[block, rows, :]
                next_dir = raw[4 + block, rows, :]
                masked = centre * sea
                up_lon = jnp.where(
                    inflow_row,
                    jnp.broadcast_to(lon_in[pl.ds(lon_base(phase) + count * t + i, 1), :], (ROWS, COLS)),
                    pltpu.roll(masked, row_shift, 0),
                )
                side = pltpu.roll(lat, (last_lane_in - j + 128) % 128, 1)
                low = pltpu.roll(masked[:, :128], lane_shift, 1)
                high = pltpu.roll(masked[:, 128:], lane_shift, 1)
                low_up = jnp.where(inflow_lane, jnp.where(up_y, side, high), low)
                high_up = jnp.where(inflow_lane, jnp.where(up_y, low, side), high)
                up_lat = jnp.concatenate([low_up, high_up], axis=1)
                speed = table[T_SPEED + freq + j]
                turning = table[T_BEND + freq + j] * bend_x
                value = sea * (
                    centre
                    - (speed * abs_cos) * (centre - up_lon)
                    - (speed * abs_sin) * (centre - up_lat)
                    - (
                        jnp.maximum(turning, 0.0) * (centre - prev_dir)
                        + jnp.minimum(turning, 0.0) * (next_dir - centre)
                    )
                )
                moved[REACH // 2 + t, first, rows, :] = value
                return steepness + table[T_STEEP + freq + j] * value

            return lax.fori_loop(0, count, one, steepness, unroll=5)

        return lax.fori_loop(0, 5 - first, one_block, steepness)

    def shifted(side, phase, action):
        rows = span(phase)
        first = (PHASES[phase][0] + side) % 2
        mine, theirs = 5 - first, 4 + first
        partner, other = (1, -1) if side == 0 else (-1, 1)

        def block_copy(start, count, step, recv):
            place = REACH + first + 2 * start - OWN * step
            return remote(
                moved.at[REACH // 2 + start : REACH // 2 + start + count, first, rows],
                moved.at[place // 2 : place // 2 + count, place % 2, rows],
                block_send,
                block_recv.at[phase, recv],
                at_comp(step),
            )

        def relay():
            start = 1 - side
            place = REACH + 1 - first + 2 * start + OWN * other
            there = place - OWN * partner
            count = theirs - 1
            return remote(
                moved.at[place // 2 : place // 2 + count, place % 2, rows],
                moved.at[there // 2 : there // 2 + count, there % 2, rows],
                block_send,
                block_recv.at[phase, 1],
                at_comp(partner),
            )

        def arrived(count, recv):
            blocks = moved.at[0:count, 0, rows]
            remote(blocks, blocks, block_send, block_recv.at[phase, recv], at_comp(1)).wait_recv()

        if action == "send":
            block_copy(side, mine - 1, other, 0).start()
            block_copy(1 - side, mine - 1, 2 * partner, 1).start()
            block_copy(0 if side else mine - 1, 1, other, 1).start()
            block_copy(0, mine, partner, 1).start()
        elif action == "relay":
            arrived(theirs - 1, 0)
            relay().start()
        else:
            arrived(theirs + 1 + 2 * (mine - 1), 1)

    def exchange(phase, action):
        for side in (0, 1):

            @pl.when(parity == side)
            def _():
                shifted(side, phase, action)

    def steep_copy(step):
        return remote(
            steep.at[comp], steep.at[comp], steep_send, steep_recv, at_comp(step)
        )

    pack(0)
    pl.semaphore_wait(barrier, 11)
    for phase in range(len(PHASES)):
        for copy in raw_copies(phase):
            copy.start()
    for phase in range(len(PHASES)):
        if phase:
            pack(phase)
        lon_copy(phase).start()
        lat_copy(phase).start()

    partial = jnp.zeros((ROWS, COLS), jnp.float32)
    for phase in range(len(PHASES)):
        wait_halos(phase)
        partial = advect(phase, partial)
        if phase < EARLY:
            exchange(phase, "send")
    steep[comp] = partial
    for step in range(1, 8):
        steep_copy(step).start()
    for phase in range(EARLY, len(PHASES)):
        exchange(phase, "send")

    weights = spread_weights()
    wind_x = (WIND_FACTOR / GRAVITY) * friction[...] * jnp.cos(wind[...])
    wind_y = (WIND_FACTOR / GRAVITY) * friction[...] * jnp.sin(wind[...])
    at_sea = sea > 0.5

    exchange(0, "relay")
    seven = steep.at[0:7]
    remote(seven, seven, steep_send, steep_recv, at_comp(1)).wait_recv()
    total = steep[0]
    for slot in range(1, 8):
        total = total + steep[slot]
    steep_loss = (TIME_STEP * STEEPNESS_LOSS) * total * total

    def sources(phase):
        upper, start, count = PHASES[phase]
        first = first_block(phase)

        def one_block(t, carry):
            block = first + 2 * t
            place = OWN * comp + block
            heading = place // 2
            freq = HALF * (place % 2)
            cos = table[T_COS + heading]
            sin = table[T_SIN + heading]
            along = cos * wind_x + sin * wind_y

            def one(i, running):
                j = start + i
                rows = pl.ds(pl.multiple_of(ROWS * j, ROWS), ROWS)
                centre = moved[REACH // 2 + t, first, rows, :]
                level = weights[0] * centre
                for m in range(1, REACH // 2 + 1):
                    level = level + weights[m] * (
                        moved[REACH // 2 + t - m, first, rows, :]
                        + moved[REACH // 2 + t + m, first, rows, :]
                    )
                excess = jnp.maximum(level - 1.0, 0.0)
                excess_sq = excess * excess
                omega = table[T_OMEGA + freq + j]
                growth = (TIME_STEP * WIND_GROWTH * omega) * jnp.maximum(omega * along - 1.0, 0.0)
                losses = omega * (
                    (TIME_STEP * SATURATION_LOSS) * excess_sq
                    + (TIME_STEP * CUMULATIVE_LOSS / NFREQ) * running
                    + steep_loss
                )
                updated = centre * (1.0 + growth) / (1.0 + losses)
                out[block, rows, :] = jnp.where(at_sea, updated, centre)
                return running + excess_sq

            if start > 0:
                before = offset[block + 1]
            elif upper:
                before = offset[block]
            else:
                before = jnp.zeros((ROWS, COLS), jnp.float32)
            offset[block + 1] = lax.fori_loop(0, count, one, before, unroll=5)
            return carry

        lax.fori_loop(0, 5 - first, one_block, 0)

    offset_copy = remote(
        offset.at[OWN], offset.at[0], offset_send, offset_recv, {"comp": comp + 1 - 2 * parity}
    )
    for phase, (upper, start, count) in enumerate(PHASES):
        if phase:
            exchange(phase, "relay")
        exchange(phase, "receive")
        if upper and start == 0:

            @pl.when(parity == 1)
            def _():
                offset_copy.wait_recv()

        sources(phase)
        if not upper and start + count == HALF:

            @pl.when(parity == 0)
            def _():
                offset_copy.start()

    @pl.when(parity == 0)
    def _():
        offset_copy.wait_send()

    for sent, sem in (
        (raw.at[0:4], raw_send),
        (lon_out, lon_send),
        (lat_out, lat_send),
        (moved.at[0:16], block_send),
        (seven, steep_send),
    ):
        remote(sent, sent, sem, raw_recv.at[0], at_comp(1)).wait_send()


def shards(spectrum, sea_mask, owner_list, owner_count, slopes, friction, wind_angle):
    blocks = spectrum.reshape(OWN, TALL, COLS)
    hbm = pl.BlockSpec(memory_space=pltpu.HBM)
    dma = pltpu.SemaphoreType.DMA
    phases = len(PHASES)
    operands = [blocks, jnp.asarray(tables()), sea_mask, slopes, friction, wind_angle]
    result = pl.pallas_call(
        kernel,
        out_shape=jax.ShapeDtypeStruct((OWN, TALL, COLS), jnp.float32),
        in_specs=[hbm] * 6,
        out_specs=pl.BlockSpec(memory_space=pltpu.VMEM),
        scratch_shapes=[
            pltpu.VMEM((OWN + 4, TALL, COLS), jnp.float32),
            pltpu.VMEM((OWN // 2 + 1 + REACH, 2, TALL, COLS), jnp.float32),
            pltpu.VMEM((lon_base(phases), COLS), jnp.float32),
            pltpu.VMEM((lon_base(phases), COLS), jnp.float32),
            pltpu.VMEM((phases, 5, ROWS, 128), jnp.float32),
            pltpu.VMEM((phases, 5, ROWS, 128), jnp.float32),
            pltpu.VMEM((8, ROWS, COLS), jnp.float32),
            pltpu.VMEM((OWN + 1, ROWS, COLS), jnp.float32),
            pltpu.SMEM((T_END,), jnp.float32),
            pltpu.VMEM((ROWS, COLS), jnp.int32),
            pltpu.VMEM((2, ROWS, COLS), jnp.float32),
            pltpu.VMEM((ROWS, COLS), jnp.float32),
            pltpu.VMEM((ROWS, COLS), jnp.float32),
            dma((6,)),
            dma,
            dma((phases,)),
            dma,
            dma((phases,)),
            dma,
            dma((phases,)),
            dma,
            dma((phases, 2)),
            dma,
            dma,
            dma,
            dma,
        ],
        compiler_params=pltpu.CompilerParams(
            collective_id=0, has_side_effects=True, vmem_limit_bytes=40 << 20
        ),
        name="wave_step",
    )(*[pltpu.with_memory_space_constraint(x, pltpu.HBM) for x in operands])
    return result.reshape(spectrum.shape)


def solution(mesh):
    in_specs = (
        P("comp", "tx", "ty"),
        P("tx", "ty"),
        P("tx", "ty", None, None),
        P("tx", "ty", None),
        P(None, "tx", "ty"),
        P("tx", "ty"),
        P("tx", "ty"),
    )
    out_specs = P("comp", "tx", "ty")
    return jax.shard_map(shards, mesh=mesh, in_specs=in_specs, out_specs=out_specs, check_vma=False)
```

```python
import math

import jax
import jax.numpy as jnp
import numpy as np
from jax import lax
from jax.experimental import pallas as pl
from jax.experimental.pallas import tpu as pltpu
from jax.sharding import PartitionSpec as P

NDIR = 36
NFREQ = 50
HALF = 25
OWN = 9
REACH = 16
ROWS = 8
COLS = 256
TALL = HALF * ROWS
PHASES = ((0, 0, 5), (0, 5, 10), (0, 15, 10), (1, 0, 10), (1, 10, 10), (1, 20, 5))
EARLY = 3

TIME_STEP = 240.0
CELL_SIZE = 11100.0
GRAVITY = 9.81
LOW_FREQ = 0.0373
HIGH_FREQ = 1.0
WIND_GROWTH = 0.0001
WIND_FACTOR = 28.0
SATURATION_LOSS = 0.0005
CUMULATIVE_LOSS = 0.001
STEEPNESS_LOSS = 0.005
SATURATION_LEVEL = 0.6

T_COS, T_SIN, T_SPEED, T_BEND, T_OMEGA, T_STEEP, T_END = 0, 36, 72, 122, 172, 222, 272


def tables():
    heading = 2.0 * math.pi / NDIR * np.arange(NDIR)
    omega = 2.0 * math.pi * LOW_FREQ * (HIGH_FREQ / LOW_FREQ) ** (np.arange(NFREQ) / (NFREQ - 1))
    speed = TIME_STEP / CELL_SIZE * GRAVITY / (2.0 * omega)
    bend = TIME_STEP * NDIR / (2.0 * math.pi) * (2.0 * math.pi * LOW_FREQ) / omega
    steep = (omega / omega[-1]) ** 2 / (NDIR * NFREQ)
    return np.concatenate([np.cos(heading), np.sin(heading), speed, bend, omega, steep]).astype(
        np.float32
    )


def spread_weights():
    weights = np.cos(2.0 * math.pi / NDIR * np.arange(REACH // 2 + 1)) ** 2
    total = weights[0] + 2.0 * np.sum(weights[1:])
    return [float(w) for w in weights / total / SATURATION_LEVEL]


def lon_rows(phase):
    return (5 * PHASES[phase][2] + ROWS - 1) // ROWS * ROWS


def lon_base(phase):
    return sum(lon_rows(p) for p in range(phase))


def kernel(
    spec,
    table_in,
    sea_in,
    slopes_in,
    friction_in,
    wind_in,
    out,
    raw,
    moved,
    lon_out,
    lon_in,
    lat_out,
    lat_in,
    steep,
    offset,
    table,
    sea_mask,
    slopes,
    friction,
    wind,
    load_sem,
    raw_send,
    raw_recv,
    lon_send,
    lon_recv,
    lat_send,
    lat_recv,
    block_send,
    block_recv,
    steep_send,
    steep_recv,
    offset_send,
    offset_recv,
):
    comp = lax.axis_index("comp")
    tx = lax.axis_index("tx")
    ty = lax.axis_index("ty")
    parity = comp % 2
    quadrant = comp // 2
    pos_x = 1 - ((quadrant + 1) // 2) % 2
    pos_y = 1 - quadrant // 2

    def at_comp(step):
        return {"comp": (comp + step + 8) % 8}

    def remote(src, dst, send, recv, device):
        return pltpu.make_async_remote_copy(
            src_ref=src,
            dst_ref=dst,
            send_sem=send,
            recv_sem=recv,
            device_id=device,
            device_id_type=pl.DeviceIdType.MESH,
        )

    barrier = pltpu.get_barrier_semaphore()

    def greet(device):
        pl.semaphore_signal(barrier, inc=1, device_id=device, device_id_type=pl.DeviceIdType.MESH)

    for step in (4, 2, 6, 1, 7):
        greet(at_comp(step))
    for step in (1, -1):
        greet({"tx": (tx + step + 8) % 8})
        greet({"ty": (ty + step + 4) % 4})

    pairs = [
        (sea_in, sea_mask),
        (spec.at[:, 0:40], raw.at[2 : 2 + OWN, 0:40]),
        (spec.at[:, 40:], raw.at[2 : 2 + OWN, 40:]),
        (table_in, table),
        (slopes_in, slopes),
        (friction_in, friction),
        (wind_in, wind),
    ]
    loads = [pltpu.make_async_copy(src, dst, load_sem.at[i]) for i, (src, dst) in enumerate(pairs)]
    for load in loads:
        load.start()

    row_ids = lax.broadcasted_iota(jnp.int32, (ROWS, COLS), 0)
    lane_ids = lax.broadcasted_iota(jnp.int32, (ROWS, 128), 1)
    inflow_row = row_ids == (1 - pos_x) * (ROWS - 1)
    last_lane_in = (1 - pos_y) * 127
    inflow_lane = lane_ids == last_lane_in
    up_y = jnp.zeros((ROWS, 128), jnp.int32) + pos_y > 0
    row_shift = jnp.where(pos_x > 0, 1, ROWS - 1)
    lane_shift = jnp.where(pos_y > 0, 1, 127)
    last_row = pos_x * (ROWS - 1)
    last_lane = pos_y * 127
    last_half = pl.multiple_of(pos_y * 128, 128)

    def first_block(phase):
        return (PHASES[phase][0] + parity) % 2

    def span(phase):
        _, start, count = PHASES[phase]
        return pl.ds(ROWS * start, ROWS * count)

    def raw_copies(phase):
        first = first_block(phase)
        rows = span(phase)
        return [
            remote(
                spec.at[first, rows],
                raw.at[11 + first, rows],
                raw_send,
                raw_recv.at[phase],
                at_comp(-1),
            ),
            remote(
                spec.at[8 - first, rows],
                raw.at[1 - first, rows],
                raw_send,
                raw_recv.at[phase],
                at_comp(1),
            ),
        ]
    pl.semaphore_wait(barrier, 9)
    for phase in range(len(PHASES)):
        for copy in raw_copies(phase):
            copy.start()
    for i, load in enumerate(loads):
        if i != 2:
            load.wait()
    sea = sea_mask[...].astype(jnp.float32)
    sea_row = jnp.sum(jnp.where(row_ids == last_row, sea, 0.0), axis=0, keepdims=True)
    sea_half = jnp.where(up_y, sea[:, 128:], sea[:, :128])

    def pack(phase):
        _, start, count = PHASES[phase]
        first = first_block(phase)

        def pack_block(t, carry):
            block = first + 2 * t

            def pack_one(i, lat):
                j = start + i
                lon_out[pl.ds(lon_base(phase) + count * t + i, 1), :] = (
                    raw[2 + block, pl.ds(ROWS * j + last_row, 1), :] * sea_row
                )
                rows = pl.ds(pl.multiple_of(ROWS * j, ROWS), ROWS)
                side = raw[2 + block, rows, pl.ds(last_half, 128)]
                turned = pltpu.roll(side * sea_half, (j - last_lane + 128) % 128, 1)
                return jnp.where(lane_ids == j, turned, lat)

            lat_out[phase, t] = lax.fori_loop(
                0, count, pack_one, jnp.zeros((ROWS, 128), jnp.float32), unroll=5
            )
            return carry

        lax.fori_loop(0, 5 - first, pack_block, 0)

    lon_to = {"tx": (tx + 2 * pos_x - 1 + 8) % 8}
    lat_to = {"ty": (ty + 2 * pos_y - 1 + 4) % 4}

    def lon_copy(phase):
        rows = pl.ds(lon_base(phase), lon_rows(phase))
        return remote(lon_out.at[rows], lon_in.at[rows], lon_send, lon_recv.at[phase], lon_to)

    def lat_copy(phase):
        return remote(lat_out.at[phase], lat_in.at[phase], lat_send, lat_recv.at[phase], lat_to)

    def wait_halos(phase):
        both = raw.at[0:2, span(phase)]
        remote(both, both, raw_send, raw_recv.at[phase], at_comp(1)).wait_recv()
        lon_copy(phase).wait_recv()
        lat_copy(phase).wait_recv()

    lat_open = jnp.where(pos_y > 0, ty, 3 - ty) > 0
    lat_gate = jnp.where(lat_open, 1.0, 0.0)
    slope_x = slopes[0]
    slope_y = slopes[1]

    def advect(phase, steepness):
        _, start, count = PHASES[phase]
        first = first_block(phase)

        def one_block(t, steepness):
            block = first + 2 * t
            place = OWN * comp + block
            heading = place // 2
            freq = HALF * (place % 2)
            cos = table[T_COS + heading]
            sin = table[T_SIN + heading]
            abs_cos = jnp.abs(cos)
            abs_sin = jnp.abs(sin)
            bend_x = sin * slope_x - cos * slope_y
            lat = lat_in[phase, t] * lat_gate

            def one(i, steepness):
                j = start + i
                rows = pl.ds(pl.multiple_of(ROWS * j, ROWS), ROWS)
                centre = raw[2 + block, rows, :]
                prev_dir = raw[block, rows, :]
                next_dir = raw[4 + block, rows, :]
                masked = centre * sea
                up_lon = jnp.where(
                    inflow_row,
                    jnp.broadcast_to(lon_in[pl.ds(lon_base(phase) + count * t + i, 1), :], (ROWS, COLS)),
                    pltpu.roll(masked, row_shift, 0),
                )
                side = pltpu.roll(lat, (last_lane_in - j + 128) % 128, 1)
                low = pltpu.roll(masked[:, :128], lane_shift, 1)
                high = pltpu.roll(masked[:, 128:], lane_shift, 1)
                low_up = jnp.where(inflow_lane, jnp.where(up_y, side, high), low)
                high_up = jnp.where(inflow_lane, jnp.where(up_y, low, side), high)
                up_lat = jnp.concatenate([low_up, high_up], axis=1)
                speed = table[T_SPEED + freq + j]
                turning = table[T_BEND + freq + j] * bend_x
                value = sea * (
                    centre
                    - (speed * abs_cos) * (centre - up_lon)
                    - (speed * abs_sin) * (centre - up_lat)
                    - (
                        jnp.maximum(turning, 0.0) * (centre - prev_dir)
                        + jnp.minimum(turning, 0.0) * (next_dir - centre)
                    )
                )
                moved[REACH // 2 + t, first, rows, :] = value
                return steepness + table[T_STEEP + freq + j] * value

            return lax.fori_loop(0, count, one, steepness, unroll=5)

        return lax.fori_loop(0, 5 - first, one_block, steepness)

    def shifted(side, phase, action):
        rows = span(phase)
        first = (PHASES[phase][0] + side) % 2
        mine, theirs = 5 - first, 4 + first
        partner, other = (1, -1) if side == 0 else (-1, 1)

        def block_copy(start, count, step, recv):
            place = REACH + first + 2 * start - OWN * step
            return remote(
                moved.at[REACH // 2 + start : REACH // 2 + start + count, first, rows],
                moved.at[place // 2 : place // 2 + count, place % 2, rows],
                block_send,
                block_recv.at[phase, recv],
                at_comp(step),
            )

        def relay():
            start = 1 - side
            place = REACH + 1 - first + 2 * start + OWN * other
            there = place - OWN * partner
            count = theirs - 1
            return remote(
                moved.at[place // 2 : place // 2 + count, place % 2, rows],
                moved.at[there // 2 : there // 2 + count, there % 2, rows],
                block_send,
                block_recv.at[phase, 1],
                at_comp(partner),
            )

        def arrived(count, recv):
            blocks = moved.at[0:count, 0, rows]
            remote(blocks, blocks, block_send, block_recv.at[phase, recv], at_comp(1)).wait_recv()

        if action == "send":
            block_copy(side, mine - 1, other, 0).start()
            block_copy(1 - side, mine - 1, 2 * partner, 1).start()
            block_copy(0 if side else mine - 1, 1, other, 1).start()
            block_copy(0, mine, partner, 1).start()
        elif action == "relay":
            arrived(theirs - 1, 0)
            relay().start()
        else:
            arrived(theirs + 1 + 2 * (mine - 1), 1)

    def exchange(phase, action):
        for side in (0, 1):

            @pl.when(parity == side)
            def _():
                shifted(side, phase, action)

    def steep_copy(src, dst, stage, step):
        return remote(steep.at[src], steep.at[dst], steep_send, steep_recv.at[stage], at_comp(step))

    def steep_wait(first, count, stage):
        blocks = steep.at[first : first + count]
        remote(blocks, blocks, steep_send, steep_recv.at[stage], at_comp(1)).wait_recv()

    def give(phase):
        pack(phase)
        lon_copy(phase).start()
        lat_copy(phase).start()

    give(0)
    loads[2].wait()
    give(1)

    partial = jnp.zeros((ROWS, COLS), jnp.float32)
    for phase in range(len(PHASES)):
        wait_halos(phase)
        partial = advect(phase, partial)
        if phase < EARLY:
            exchange(phase, "send")
        if phase + 2 < len(PHASES):
            give(phase + 2)
    steep[0] = partial

    @pl.when(parity == 1)
    def _():
        steep_copy(0, 1, 0, -1).start()

    @pl.when(parity == 0)
    def _():
        steep_wait(1, 1, 0)
        steep[2] = steep[0] + steep[1]
        for i in range(3):
            steep_copy(2, 3 + i, 1, 2 * i + 2).start()

    for phase in range(EARLY, len(PHASES)):
        exchange(phase, "send")

    weights = spread_weights()
    wind_x = (WIND_FACTOR / GRAVITY) * friction[...] * jnp.cos(wind[...])
    wind_y = (WIND_FACTOR / GRAVITY) * friction[...] * jnp.sin(wind[...])
    at_sea = sea > 0.5

    exchange(0, "relay")

    @pl.when(parity == 0)
    def _():
        steep_wait(3, 3, 1)
        steep[6] = (steep[2] + steep[4]) + (steep[3] + steep[5])
        steep_copy(6, 6, 2, 1).start()

    @pl.when(parity == 1)
    def _():
        steep_wait(6, 1, 2)

    total = steep[6]
    steep_loss = (TIME_STEP * STEEPNESS_LOSS) * total * total

    def sources(phase):
        upper, start, count = PHASES[phase]
        first = first_block(phase)

        def one_block(t, carry):
            block = first + 2 * t
            place = OWN * comp + block
            heading = place // 2
            freq = HALF * (place % 2)
            cos = table[T_COS + heading]
            sin = table[T_SIN + heading]
            along = cos * wind_x + sin * wind_y

            def one(i, running):
                j = start + i
                rows = pl.ds(pl.multiple_of(ROWS * j, ROWS), ROWS)
                centre = moved[REACH // 2 + t, first, rows, :]
                level = weights[0] * centre
                for m in range(1, REACH // 2 + 1):
                    level = level + weights[m] * (
                        moved[REACH // 2 + t - m, first, rows, :]
                        + moved[REACH // 2 + t + m, first, rows, :]
                    )
                excess = jnp.maximum(level - 1.0, 0.0)
                excess_sq = excess * excess
                omega = table[T_OMEGA + freq + j]
                growth = (TIME_STEP * WIND_GROWTH * omega) * jnp.maximum(omega * along - 1.0, 0.0)
                losses = omega * (
                    (TIME_STEP * SATURATION_LOSS) * excess_sq
                    + (TIME_STEP * CUMULATIVE_LOSS / NFREQ) * running
                    + steep_loss
                )
                updated = centre * (1.0 + growth) / (1.0 + losses)
                out[block, rows, :] = jnp.where(at_sea, updated, centre)
                return running + excess_sq

            if start > 0:
                before = offset[block + 1]
            elif upper:
                before = offset[block]
            else:
                before = jnp.zeros((ROWS, COLS), jnp.float32)
            offset[block + 1] = lax.fori_loop(0, count, one, before, unroll=5)
            return carry

        lax.fori_loop(0, 5 - first, one_block, 0)

    offset_copy = remote(
        offset.at[OWN], offset.at[0], offset_send, offset_recv, {"comp": comp + 1 - 2 * parity}
    )
    for phase, (upper, start, count) in enumerate(PHASES):
        if phase:
            exchange(phase, "relay")
        exchange(phase, "receive")
        if upper and start == 0:

            @pl.when(parity == 1)
            def _():
                offset_copy.wait_recv()

        sources(phase)
        if not upper and start + count == HALF:

            @pl.when(parity == 0)
            def _():
                offset_copy.start()

    @pl.when(parity == 0)
    def _():
        offset_copy.wait_send()

    for sent, sem in (
        (raw.at[0:4], raw_send),
        (lon_out, lon_send),
        (lat_out, lat_send),
        (moved.at[0:16], block_send),
    ):
        remote(sent, sent, sem, raw_recv.at[0], at_comp(1)).wait_send()
    for side, count in ((0, 4), (1, 1)):

        @pl.when(parity == side)
        def _():
            sums = steep.at[0:count]
            remote(sums, sums, steep_send, raw_recv.at[0], at_comp(1)).wait_send()


def shards(spectrum, sea_mask, owner_list, owner_count, slopes, friction, wind_angle):
    blocks = spectrum.reshape(OWN, TALL, COLS)
    hbm = pl.BlockSpec(memory_space=pltpu.HBM)
    dma = pltpu.SemaphoreType.DMA
    phases = len(PHASES)
    operands = [blocks, jnp.asarray(tables()), sea_mask, slopes, friction, wind_angle]
    result = pl.pallas_call(
        kernel,
        out_shape=jax.ShapeDtypeStruct((OWN, TALL, COLS), jnp.float32),
        in_specs=[hbm] * 6,
        out_specs=pl.BlockSpec(memory_space=pltpu.VMEM),
        scratch_shapes=[
            pltpu.VMEM((OWN + 4, TALL, COLS), jnp.float32),
            pltpu.VMEM((OWN // 2 + 1 + REACH, 2, TALL, COLS), jnp.float32),
            pltpu.VMEM((lon_base(phases), COLS), jnp.float32),
            pltpu.VMEM((lon_base(phases), COLS), jnp.float32),
            pltpu.VMEM((phases, 5, ROWS, 128), jnp.float32),
            pltpu.VMEM((phases, 5, ROWS, 128), jnp.float32),
            pltpu.VMEM((8, ROWS, COLS), jnp.float32),
            pltpu.VMEM((OWN + 1, ROWS, COLS), jnp.float32),
            pltpu.SMEM((T_END,), jnp.float32),
            pltpu.VMEM((ROWS, COLS), jnp.int32),
            pltpu.VMEM((2, ROWS, COLS), jnp.float32),
            pltpu.VMEM((ROWS, COLS), jnp.float32),
            pltpu.VMEM((ROWS, COLS), jnp.float32),
            dma((7,)),
            dma,
            dma((phases,)),
            dma,
            dma((phases,)),
            dma,
            dma((phases,)),
            dma,
            dma((phases, 2)),
            dma,
            dma((3,)),
            dma,
            dma,
        ],
        compiler_params=pltpu.CompilerParams(
            collective_id=0, has_side_effects=True, vmem_limit_bytes=40 << 20
        ),
        name="wave_step",
    )(*[pltpu.with_memory_space_constraint(x, pltpu.HBM) for x in operands])
    return result.reshape(spectrum.shape)


def solution(mesh):
    in_specs = (
        P("comp", "tx", "ty"),
        P("tx", "ty"),
        P("tx", "ty", None, None),
        P("tx", "ty", None),
        P(None, "tx", "ty"),
        P("tx", "ty"),
        P("tx", "ty"),
    )
    out_specs = P("comp", "tx", "ty")
    return jax.shard_map(shards, mesh=mesh, in_specs=in_specs, out_specs=out_specs, check_vma=False)
```

```python
import math

import jax
import jax.numpy as jnp
import numpy as np
from jax import lax
from jax.experimental import pallas as pl
from jax.experimental.pallas import tpu as pltpu
from jax.sharding import PartitionSpec as P

NDIR = 36
NFREQ = 50
HALF = 25
OWN = 9
REACH = 16
ROWS = 8
COLS = 256
TALL = HALF * ROWS
PHASES = ((0, 0, 5), (0, 5, 10), (0, 15, 10), (1, 0, 10), (1, 10, 10), (1, 20, 5))
EARLY = 3

TIME_STEP = 240.0
CELL_SIZE = 11100.0
GRAVITY = 9.81
LOW_FREQ = 0.0373
HIGH_FREQ = 1.0
WIND_GROWTH = 0.0001
WIND_FACTOR = 28.0
SATURATION_LOSS = 0.0005
CUMULATIVE_LOSS = 0.001
STEEPNESS_LOSS = 0.005
SATURATION_LEVEL = 0.6

T_COS, T_SIN, T_SPEED, T_BEND, T_OMEGA, T_STEEP, T_END = 0, 36, 72, 122, 172, 222, 272


def tables():
    heading = 2.0 * math.pi / NDIR * np.arange(NDIR)
    omega = 2.0 * math.pi * LOW_FREQ * (HIGH_FREQ / LOW_FREQ) ** (np.arange(NFREQ) / (NFREQ - 1))
    speed = TIME_STEP / CELL_SIZE * GRAVITY / (2.0 * omega)
    bend = TIME_STEP * NDIR / (2.0 * math.pi) * (2.0 * math.pi * LOW_FREQ) / omega
    steep = (omega / omega[-1]) ** 2 / (NDIR * NFREQ)
    return np.concatenate([np.cos(heading), np.sin(heading), speed, bend, omega, steep]).astype(
        np.float32
    )


def spread_weights():
    weights = np.cos(2.0 * math.pi / NDIR * np.arange(REACH // 2 + 1)) ** 2
    total = weights[0] + 2.0 * np.sum(weights[1:])
    return [float(w) for w in weights / total / SATURATION_LEVEL]


def lon_rows(phase):
    return (5 * PHASES[phase][2] + ROWS - 1) // ROWS * ROWS


def lon_base(phase):
    return sum(lon_rows(p) for p in range(phase))


def kernel(
    spec,
    table_in,
    sea_in,
    slopes_in,
    friction_in,
    wind_in,
    out,
    raw,
    moved,
    lon_out,
    lon_in,
    lat_out,
    lat_in,
    steep,
    offset,
    table,
    sea_mask,
    slopes,
    friction,
    wind,
    load_sem,
    raw_send,
    raw_recv,
    lon_send,
    lon_recv,
    lat_send,
    lat_recv,
    block_send,
    block_recv,
    steep_send,
    steep_recv,
    offset_send,
    offset_recv,
):
    comp = lax.axis_index("comp")
    tx = lax.axis_index("tx")
    ty = lax.axis_index("ty")
    parity = comp % 2
    quadrant = comp // 2
    pos_x = 1 - ((quadrant + 1) // 2) % 2
    pos_y = 1 - quadrant // 2

    def at_comp(step):
        return {"comp": (comp + step + 8) % 8}

    def remote(src, dst, send, recv, device):
        return pltpu.make_async_remote_copy(
            src_ref=src,
            dst_ref=dst,
            send_sem=send,
            recv_sem=recv,
            device_id=device,
            device_id_type=pl.DeviceIdType.MESH,
        )

    barrier = pltpu.get_barrier_semaphore()

    def greet(device):
        pl.semaphore_signal(barrier, inc=1, device_id=device, device_id_type=pl.DeviceIdType.MESH)

    for step in (4, 2, 6, 1, 7):
        greet(at_comp(step))
    for step in (1, -1):
        greet({"tx": (tx + step + 8) % 8})
        greet({"ty": (ty + step + 4) % 4})

    pairs = [
        (sea_in, sea_mask),
        (spec.at[:, 0:40], raw.at[2 : 2 + OWN, 0:40]),
        (spec.at[:, 40:], raw.at[2 : 2 + OWN, 40:]),
        (table_in, table),
        (slopes_in, slopes),
        (friction_in, friction),
        (wind_in, wind),
    ]
    loads = [pltpu.make_async_copy(src, dst, load_sem.at[i]) for i, (src, dst) in enumerate(pairs)]
    for load in loads:
        load.start()

    row_ids = lax.broadcasted_iota(jnp.int32, (ROWS, COLS), 0)
    lane_ids = lax.broadcasted_iota(jnp.int32, (ROWS, 128), 1)
    inflow_row = row_ids == (1 - pos_x) * (ROWS - 1)
    last_lane_in = (1 - pos_y) * 127
    inflow_lane = lane_ids == last_lane_in
    up_y = jnp.zeros((ROWS, 128), jnp.int32) + pos_y > 0
    row_shift = jnp.where(pos_x > 0, 1, ROWS - 1)
    lane_shift = jnp.where(pos_y > 0, 1, 127)
    last_row = pos_x * (ROWS - 1)
    last_lane = pos_y * 127
    last_half = pl.multiple_of(pos_y * 128, 128)

    def first_block(phase):
        return (PHASES[phase][0] + parity) % 2

    def span(phase):
        _, start, count = PHASES[phase]
        return pl.ds(ROWS * start, ROWS * count)

    def raw_copies(phase):
        first = first_block(phase)
        rows = span(phase)
        return [
            remote(
                spec.at[first, rows],
                raw.at[11 + first, rows],
                raw_send,
                raw_recv.at[phase],
                at_comp(-1),
            ),
            remote(
                spec.at[8 - first, rows],
                raw.at[1 - first, rows],
                raw_send,
                raw_recv.at[phase],
                at_comp(1),
            ),
        ]
    pl.semaphore_wait(barrier, 9)
    for phase in range(len(PHASES)):
        for copy in raw_copies(phase):
            copy.start()
    for i, load in enumerate(loads):
        if i != 2:
            load.wait()
    sea = sea_mask[...].astype(jnp.float32)
    sea_row = jnp.sum(jnp.where(row_ids == last_row, sea, 0.0), axis=0, keepdims=True)
    sea_half = jnp.where(up_y, sea[:, 128:], sea[:, :128])

    def pack(phase):
        _, start, count = PHASES[phase]
        first = first_block(phase)

        def pack_block(t, carry):
            block = first + 2 * t

            def pack_one(i, lat):
                j = start + i
                lon_out[pl.ds(lon_base(phase) + count * t + i, 1), :] = (
                    raw[2 + block, pl.ds(ROWS * j + last_row, 1), :] * sea_row
                )
                rows = pl.ds(pl.multiple_of(ROWS * j, ROWS), ROWS)
                side = raw[2 + block, rows, pl.ds(last_half, 128)]
                turned = pltpu.roll(side * sea_half, (j - last_lane + 128) % 128, 1)
                return jnp.where(lane_ids == j, turned, lat)

            lat_out[phase, t] = lax.fori_loop(
                0, count, pack_one, jnp.zeros((ROWS, 128), jnp.float32), unroll=5
            )
            return carry

        lax.fori_loop(0, 5 - first, pack_block, 0)

    lon_to = {"tx": (tx + 2 * pos_x - 1 + 8) % 8}
    lat_to = {"ty": (ty + 2 * pos_y - 1 + 4) % 4}

    def lon_copy(phase):
        rows = pl.ds(lon_base(phase), lon_rows(phase))
        return remote(lon_out.at[rows], lon_in.at[rows], lon_send, lon_recv.at[phase], lon_to)

    def lat_copy(phase):
        return remote(lat_out.at[phase], lat_in.at[phase], lat_send, lat_recv.at[phase], lat_to)

    def wait_halos(phase):
        both = raw.at[0:2, span(phase)]
        remote(both, both, raw_send, raw_recv.at[phase], at_comp(1)).wait_recv()
        lon_copy(phase).wait_recv()
        lat_copy(phase).wait_recv()

    lat_open = jnp.where(pos_y > 0, ty, 3 - ty) > 0
    lat_gate = jnp.where(lat_open, 1.0, 0.0)
    slope_x = slopes[0]
    slope_y = slopes[1]

    def advect(phase, steepness):
        _, start, count = PHASES[phase]
        first = first_block(phase)

        def one_block(t, steepness):
            block = first + 2 * t
            place = OWN * comp + block
            heading = place // 2
            freq = HALF * (place % 2)
            cos = table[T_COS + heading]
            sin = table[T_SIN + heading]
            abs_cos = jnp.abs(cos)
            abs_sin = jnp.abs(sin)
            bend_x = sin * slope_x - cos * slope_y
            lat = lat_in[phase, t] * lat_gate

            def one(i, steepness):
                j = start + i
                rows = pl.ds(pl.multiple_of(ROWS * j, ROWS), ROWS)
                centre = raw[2 + block, rows, :]
                prev_dir = raw[block, rows, :]
                next_dir = raw[4 + block, rows, :]
                masked = centre * sea
                up_lon = jnp.where(
                    inflow_row,
                    jnp.broadcast_to(lon_in[pl.ds(lon_base(phase) + count * t + i, 1), :], (ROWS, COLS)),
                    pltpu.roll(masked, row_shift, 0),
                )
                side = pltpu.roll(lat, (last_lane_in - j + 128) % 128, 1)
                low = pltpu.roll(masked[:, :128], lane_shift, 1)
                high = pltpu.roll(masked[:, 128:], lane_shift, 1)
                low_up = jnp.where(inflow_lane, jnp.where(up_y, side, high), low)
                high_up = jnp.where(inflow_lane, jnp.where(up_y, low, side), high)
                up_lat = jnp.concatenate([low_up, high_up], axis=1)
                speed = table[T_SPEED + freq + j]
                turning = table[T_BEND + freq + j] * bend_x
                value = sea * (
                    centre
                    - (speed * abs_cos) * (centre - up_lon)
                    - (speed * abs_sin) * (centre - up_lat)
                    - (
                        jnp.maximum(turning, 0.0) * (centre - prev_dir)
                        + jnp.minimum(turning, 0.0) * (next_dir - centre)
                    )
                )
                moved[REACH // 2 + t, first, rows, :] = value
                return steepness + table[T_STEEP + freq + j] * value

            return lax.fori_loop(0, count, one, steepness, unroll=5)

        return lax.fori_loop(0, 5 - first, one_block, steepness)

    def shifted(side, phase, action):
        rows = span(phase)
        first = (PHASES[phase][0] + side) % 2
        mine, theirs = 5 - first, 4 + first
        partner, other = (1, -1) if side == 0 else (-1, 1)

        def block_copy(start, count, step, recv):
            place = REACH + first + 2 * start - OWN * step
            return remote(
                moved.at[REACH // 2 + start : REACH // 2 + start + count, first, rows],
                moved.at[place // 2 : place // 2 + count, place % 2, rows],
                block_send,
                block_recv.at[phase, recv],
                at_comp(step),
            )

        def relay():
            start = 1 - side
            place = REACH + 1 - first + 2 * start + OWN * other
            there = place - OWN * partner
            count = theirs - 1
            return remote(
                moved.at[place // 2 : place // 2 + count, place % 2, rows],
                moved.at[there // 2 : there // 2 + count, there % 2, rows],
                block_send,
                block_recv.at[phase, 1],
                at_comp(partner),
            )

        def arrived(count, recv):
            blocks = moved.at[0:count, 0, rows]
            remote(blocks, blocks, block_send, block_recv.at[phase, recv], at_comp(1)).wait_recv()

        if action == "send":
            block_copy(side, mine - 1, other, 0).start()
            block_copy(1 - side, mine - 1, 2 * partner, 1).start()
            block_copy(0 if side else mine - 1, 1, other, 1).start()
            block_copy(0, mine, partner, 1).start()
        elif action == "relay":
            arrived(theirs - 1, 0)
            relay().start()
        else:
            arrived(theirs + 1 + 2 * (mine - 1), 1)

    def exchange(phase, action):
        for side in (0, 1):

            @pl.when(parity == side)
            def _():
                shifted(side, phase, action)

    def steep_copy(src, dst, stage, step):
        return remote(steep.at[src], steep.at[dst], steep_send, steep_recv.at[stage], at_comp(step))

    def steep_wait(first, count, stage):
        blocks = steep.at[first : first + count]
        remote(blocks, blocks, steep_send, steep_recv.at[stage], at_comp(1)).wait_recv()

    def give(phase):
        pack(phase)
        lon_copy(phase).start()
        lat_copy(phase).start()

    give(0)
    loads[2].wait()
    give(1)

    partial = jnp.zeros((ROWS, COLS), jnp.float32)
    for phase in range(len(PHASES)):
        wait_halos(phase)
        partial = advect(phase, partial)
        if phase < EARLY:
            exchange(phase, "send")
        if phase + 2 < len(PHASES):
            give(phase + 2)
    steep[0] = partial

    @pl.when(parity == 1)
    def _():
        steep_copy(0, 1, 0, -1).start()

    @pl.when(parity == 0)
    def _():
        steep_wait(1, 1, 0)
        steep[2] = steep[0] + steep[1]
        for i in range(3):
            steep_copy(2, 3 + i, 1, 2 * i + 2).start()

    for phase in range(EARLY, len(PHASES)):
        exchange(phase, "send")

    weights = spread_weights()
    wind_x = (WIND_FACTOR / GRAVITY) * friction[...] * jnp.cos(wind[...])
    wind_y = (WIND_FACTOR / GRAVITY) * friction[...] * jnp.sin(wind[...])
    at_sea = sea > 0.5

    exchange(0, "relay")

    @pl.when(parity == 0)
    def _():
        steep_wait(3, 3, 1)
        steep[6] = (steep[2] + steep[4]) + (steep[3] + steep[5])
        steep_copy(6, 6, 2, 1).start()

    @pl.when(parity == 1)
    def _():
        steep_wait(6, 1, 2)

    total = steep[6]
    steep_loss = (TIME_STEP * STEEPNESS_LOSS) * total * total

    def sources(phase):
        upper, start, count = PHASES[phase]
        first = first_block(phase)

        def one_block(t, carry):
            block = first + 2 * t
            place = OWN * comp + block
            heading = place // 2
            freq = HALF * (place % 2)
            cos = table[T_COS + heading]
            sin = table[T_SIN + heading]
            along = cos * wind_x + sin * wind_y

            def one(i, running):
                j = start + i
                rows = pl.ds(pl.multiple_of(ROWS * j, ROWS), ROWS)
                centre = moved[REACH // 2 + t, first, rows, :]
                level = weights[0] * centre
                for m in range(1, REACH // 2 + 1):
                    level = level + weights[m] * (
                        moved[REACH // 2 + t - m, first, rows, :]
                        + moved[REACH // 2 + t + m, first, rows, :]
                    )
                excess = jnp.maximum(level - 1.0, 0.0)
                excess_sq = excess * excess
                omega = table[T_OMEGA + freq + j]
                growth = (TIME_STEP * WIND_GROWTH * omega) * jnp.maximum(omega * along - 1.0, 0.0)
                losses = omega * (
                    (TIME_STEP * SATURATION_LOSS) * excess_sq
                    + (TIME_STEP * CUMULATIVE_LOSS / NFREQ) * running
                    + steep_loss
                )
                updated = centre * (1.0 + growth) / (1.0 + losses)
                out[block, rows, :] = jnp.where(at_sea, updated, centre)
                return running + excess_sq

            if start > 0:
                before = offset[block + 1]
            elif upper:
                before = offset[block]
            else:
                before = jnp.zeros((ROWS, COLS), jnp.float32)
            offset[block + 1] = lax.fori_loop(0, count, one, before, unroll=count)
            return carry

        lax.fori_loop(0, 5 - first, one_block, 0)

    offset_copy = remote(
        offset.at[OWN], offset.at[0], offset_send, offset_recv, {"comp": comp + 1 - 2 * parity}
    )
    for phase, (upper, start, count) in enumerate(PHASES):
        if phase:
            exchange(phase, "relay")
        exchange(phase, "receive")
        if upper and start == 0:

            @pl.when(parity == 1)
            def _():
                offset_copy.wait_recv()

        sources(phase)
        if not upper and start + count == HALF:

            @pl.when(parity == 0)
            def _():
                offset_copy.start()

    @pl.when(parity == 0)
    def _():
        offset_copy.wait_send()

    for sent, sem in (
        (raw.at[0:4], raw_send),
        (lon_out, lon_send),
        (lat_out, lat_send),
        (moved.at[0:16], block_send),
    ):
        remote(sent, sent, sem, raw_recv.at[0], at_comp(1)).wait_send()
    for side, count in ((0, 4), (1, 1)):

        @pl.when(parity == side)
        def _():
            sums = steep.at[0:count]
            remote(sums, sums, steep_send, raw_recv.at[0], at_comp(1)).wait_send()


def shards(spectrum, sea_mask, owner_list, owner_count, slopes, friction, wind_angle):
    blocks = spectrum.reshape(OWN, TALL, COLS)
    hbm = pl.BlockSpec(memory_space=pltpu.HBM)
    dma = pltpu.SemaphoreType.DMA
    phases = len(PHASES)
    operands = [blocks, jnp.asarray(tables()), sea_mask, slopes, friction, wind_angle]
    result = pl.pallas_call(
        kernel,
        out_shape=jax.ShapeDtypeStruct((OWN, TALL, COLS), jnp.float32),
        in_specs=[hbm] * 6,
        out_specs=pl.BlockSpec(memory_space=pltpu.VMEM),
        scratch_shapes=[
            pltpu.VMEM((OWN + 4, TALL, COLS), jnp.float32),
            pltpu.VMEM((OWN // 2 + 1 + REACH, 2, TALL, COLS), jnp.float32),
            pltpu.VMEM((lon_base(phases), COLS), jnp.float32),
            pltpu.VMEM((lon_base(phases), COLS), jnp.float32),
            pltpu.VMEM((phases, 5, ROWS, 128), jnp.float32),
            pltpu.VMEM((phases, 5, ROWS, 128), jnp.float32),
            pltpu.VMEM((8, ROWS, COLS), jnp.float32),
            pltpu.VMEM((OWN + 1, ROWS, COLS), jnp.float32),
            pltpu.SMEM((T_END,), jnp.float32),
            pltpu.VMEM((ROWS, COLS), jnp.int32),
            pltpu.VMEM((2, ROWS, COLS), jnp.float32),
            pltpu.VMEM((ROWS, COLS), jnp.float32),
            pltpu.VMEM((ROWS, COLS), jnp.float32),
            dma((7,)),
            dma,
            dma((phases,)),
            dma,
            dma((phases,)),
            dma,
            dma((phases,)),
            dma,
            dma((phases, 2)),
            dma,
            dma((3,)),
            dma,
            dma,
        ],
        compiler_params=pltpu.CompilerParams(
            collective_id=0, has_side_effects=True, vmem_limit_bytes=40 << 20
        ),
        name="wave_step",
    )(*[pltpu.with_memory_space_constraint(x, pltpu.HBM) for x in operands])
    return result.reshape(spectrum.shape)


def solution(mesh):
    in_specs = (
        P("comp", "tx", "ty"),
        P("tx", "ty"),
        P("tx", "ty", None, None),
        P("tx", "ty", None),
        P(None, "tx", "ty"),
        P("tx", "ty"),
        P("tx", "ty"),
    )
    out_specs = P("comp", "tx", "ty")
    return jax.shard_map(shards, mesh=mesh, in_specs=in_specs, out_specs=out_specs, check_vma=False)
```
